32 devices in a mesh: replica: 8 (over z, x), expert: 4 (over y, core).
Axes of the slice: x: 2, y: 2, z: 4, core: 2. Of those that a mesh axis runs over, the one named last changes fastest.
Arguments:
- weights: bfloat16 [4, 2048, 512], P('expert'), may hold values from -3 to 3
- momentum: float32 [8, 4, 2048, 512], P('replica', 'expert'), may hold values from -6 to 6
- gradients: bfloat16 [2, 8, 4, 2048, 512], P(None, 'replica', 'expert'), may hold values from -6 to 6
- outer_momentum: float32 [4, 2048, 512], P('expert', 'replica'), may hold values from -2 to 2
Outputs:
- new_weights: bfloat16 [4, 2048, 512], P('expert')
- new_outer: float32 [4, 2048, 512], P('expert', 'replica')
The draws below stay inside these ranges and needn't reach their ends.
All inputs are finite; a program needn't handle non-finite values.
Results may differ from the reference program's by a relative error of at most 0.0075.
Values may be sent and summed in bfloat16 or wider, within the bound.
No kernel may reach another device: no remote copies, remote signals or barrier semaphores. Data moves between devices by JAX's collectives and lax.ppermute only.
A program may use at most 64 MiB of HBM per device.

```python
import math
import jax
import jax.numpy as jnp
import numpy as np
from jax import lax

ROWS = 2048
COLS = 512
STEPS = 2
NS_ITERS = 3
EXPERTS = 4
REPLICAS = 8


def block_scale(rng, extent, pieces, low, largest):
    level, own = 1.0, jax.random.fold_in(rng, 6)
    for dim, shards_of in pieces:
        draws = jnp.exp(jax.random.uniform(jax.random.fold_in(own, dim), (shards_of,), jnp.float32, low / len(pieces), largest / len(pieces)))
        level = level * jnp.repeat(draws, extent[dim] // shards_of).reshape([-1 if axis == dim else 1 for axis in range(len(extent))])
    return level


def normal_values(rng, shape, scale, reach, split=(), kind=jnp.bfloat16):
    entries = jax.random.normal(rng, shape, jnp.float32) * scale
    if len(split) > 0:
        entries = block_scale(rng, shape, split, -0.22, 0.18) * entries
    return jnp.clip(entries, min=-reach, max=reach).astype(kind)


def setup_inputs(seed: int = 0) -> dict:
    key_of = jax.random.split(jax.random.key(seed), 5)
    weights = normal_values(key_of[0], (EXPERTS, ROWS, COLS), 0.5, 3.0, ((0, 4),))
    momentum = normal_values(key_of[1], (REPLICAS, EXPERTS, ROWS, COLS), 1.0, 6.0, ((0, 8), (1, 4)), jnp.float32)
    gradients = normal_values(key_of[2], (STEPS, REPLICAS, EXPERTS, ROWS, COLS), 1.0, 6.0, ((1, 8), (2, 4)))
    outer_momentum = normal_values(key_of[3], (EXPERTS, ROWS, COLS), 0.3, 2.0, ((0, 4), (1, 8)), jnp.float32)
    return dict(weights=weights, momentum=momentum, gradients=gradients, outer_momentum=outer_momentum)


coef_a = 3.4445
coef_b = -4.775
coef_c = 2.0315
inner_beta = 0.9
outer_beta = 0.9
outer_rate = 1.0
epsilon = 1e-07

def dot_high(left, right):
    return jnp.dot(left, right, precision=lax.Precision.HIGHEST, preferred_element_type=jnp.float32)

def orthogonal(matrix):
    norm_value = jnp.sqrt(jnp.sum(matrix * matrix))
    current = (matrix / (norm_value + epsilon)).astype(jnp.bfloat16)
    for index in range(NS_ITERS):
        wide = current.astype(jnp.float32)
        gram = dot_high(wide.T, wide).astype(jnp.bfloat16).astype(jnp.float32)
        poly = (coef_b * gram + coef_c * dot_high(gram, gram)).astype(jnp.bfloat16).astype(jnp.float32)
        current = (coef_a * wide + dot_high(wide, poly)).astype(jnp.bfloat16)
    return current

def per_expert(items):
    start, moment, grads, outer = items
    update_scale = 0.5 * 0.2 * math.sqrt(ROWS)
    local = jnp.broadcast_to(start[None], moment.shape).astype(jnp.bfloat16)
    for step in range(STEPS):
        partner = np.arange(REPLICAS) ^ 1 << step
        moment = inner_beta * moment + grads[step].astype(jnp.float32)
        moment = 0.5 * (moment + moment[partner])
        ortho = lax.map(orthogonal, moment)
        local = (local.astype(jnp.float32) - update_scale * ortho.astype(jnp.float32)).astype(jnp.bfloat16)
    delta = lax.optimization_barrier(jnp.sum(start.astype(jnp.float32)[None] - local.astype(jnp.float32), axis=0)) / REPLICAS
    fresh = outer_beta * outer + delta
    result = (start.astype(jnp.float32) - outer_rate * fresh).astype(jnp.bfloat16)
    return (result, fresh)

def reference(weights, momentum, gradients, outer_momentum):
    moments = jnp.moveaxis(momentum, 1, 0)
    grads = jnp.moveaxis(gradients, 2, 0)
    new_weights, new_outer = lax.map(per_expert, (weights, moments, grads, outer_momentum))
    return (new_weights, new_outer)
```

```python
import functools
import math

import jax
import jax.numpy as jnp
from jax import lax
from jax.experimental import pallas as pl
from jax.experimental.pallas import tpu as pltpu
from jax.sharding import PartitionSpec as P

AXIS = "replica"
CHUNKS = 8
LAG = 2

coef_a = 3.4445
coef_b = -4.775
coef_c = 2.0315
inner_beta = 0.9
outer_beta = 0.9
outer_rate = 1.0
epsilon = 1e-07

BF = jnp.bfloat16
F32 = jnp.float32


def swap(block, mask):
    count = lax.axis_size(AXIS)
    return lax.ppermute(block, AXIS, [(i, i ^ mask) for i in range(count)])


def gram_of(block):
    return lax.dot_general(
        block, block, (((0,), (0,)), ((), ())), preferred_element_type=F32
    )


def dot(left, right):
    return jnp.dot(left, right, preferred_element_type=F32)


def whole(shape):
    return pl.BlockSpec(shape, lambda i: (0,) * len(shape))


ANY = pl.BlockSpec(memory_space=pl.ANY)


def cost(flops, nbytes):
    return pl.CostEstimate(flops=int(flops), bytes_accessed=int(nbytes), transcendentals=0)


def prep_body(count, *refs):
    ins, outs = refs[: 2 * count], refs[2 * count :]
    for i in range(count):
        outs[i][...] = (
            inner_beta * ins[2 * i][...] + ins[2 * i + 1][...].astype(F32)
        ).astype(BF)


def prepare(moment, grads, chunks):
    rows, cols = moment.shape
    n = rows // CHUNKS
    specs, args = [], []
    for k in chunks:
        specs.append(pl.BlockSpec((n, cols), lambda i, k=k: (k, 0)))
        specs.append(pl.BlockSpec((None, n, cols), lambda i, k=k: (0, k, 0)))
        args += [moment, grads]
    return pl.pallas_call(
        functools.partial(prep_body, len(chunks)),
        grid=(1,),
        out_shape=[jax.ShapeDtypeStruct((n, cols), BF)] * len(chunks),
        in_specs=specs,
        out_specs=[whole((n, cols))] * len(chunks),
        cost_estimate=cost(2 * n * cols * len(chunks), 8 * n * cols * len(chunks)),
        name="prep",
    )(*args)


def tick_body(first, last, names, *refs):
    ref = dict(zip(names, refs))
    if first:
        mean = 0.5 * (ref["own0"][...].astype(F32) + ref["got0"][...].astype(F32))
        low = mean.astype(BF)
        ref["m0"][...] = low
        ref["send"][...] = (inner_beta * mean + ref["grad"][...].astype(F32)).astype(BF)
        gram = gram_of(low)
        ref["g0"][...] = gram + ref["g0in"][...] if "g0in" in ref else gram
    if last:
        low = (
            0.5 * (ref["own1"][...].astype(F32) + ref["got1"][...].astype(F32))
        ).astype(BF)
        ref["m1"][...] = low
        gram = gram_of(low)
        ref["g1"][...] = gram + ref["g1in"][...] if "g1in" in ref else gram


def tick(j, state, grads):
    rows, cols = state["rows"], state["cols"]
    n = rows // CHUNKS
    chunk = whole((n, cols))
    square = whole((cols, cols))
    names, specs, args = [], [], []
    onames, ospecs, oshapes = [], [], []
    alias = {}

    def put(name, spec, value):
        names.append(name)
        specs.append(spec)
        args.append(value)

    def out(name, spec, shape, dtype, onto=None):
        if onto is not None:
            alias[names.index(onto)] = len(onames)
        onames.append(name)
        ospecs.append(spec)
        oshapes.append(jax.ShapeDtypeStruct(shape, dtype))

    first, last = j < CHUNKS, j >= LAG
    if first:
        put("own0", chunk, state["own0"][j])
        put("got0", chunk, state["got0"][j])
        put("grad", pl.BlockSpec((None, n, cols), lambda i: (1, j, 0)), grads)
        if j > 0:
            put("g0in", square, state["g0"])
            put("m0in", ANY, state["m0"])
    if last:
        i = j - LAG
        put("own1", chunk, state["own1"][i])
        put("got1", chunk, state["got1"][i])
        if i > 0:
            put("g1in", square, state["g1"])
            put("m1in", ANY, state["m1"])
    if first:
        place = pl.BlockSpec((n, cols), lambda i: (j, 0))
        out("m0", place, (rows, cols), BF, "m0in" if j > 0 else None)
        out("send", chunk, (n, cols), BF)
        out("g0", square, (cols, cols), F32, "g0in" if j > 0 else None)
    if last:
        place = pl.BlockSpec((n, cols), lambda i: (j - LAG, 0))
        out("m1", place, (rows, cols), BF, "m1in" if i > 0 else None)
        out("g1", square, (cols, cols), F32, "g1in" if i > 0 else None)
    results = pl.pallas_call(
        functools.partial(tick_body, first, last, names + onames),
        grid=(1,),
        out_shape=oshapes,
        in_specs=specs,
        out_specs=ospecs,
        input_output_aliases=alias,
        cost_estimate=cost(4 * n * cols * cols, 8 * cols * cols + 10 * n * cols),
        name="tick",
    )(*args)
    got = dict(zip(onames, results))
    if first:
        state["own1"].append(got.pop("send"))
    state.update(got)


def ortho_body(share, groups, flips, gram_ref, m_ref, *outs):
    gram = gram_ref[...]
    size = gram.shape[0]
    eye = lax.broadcasted_iota(jnp.int32, (size, size), 0) == lax.broadcasted_iota(
        jnp.int32, (size, size), 1
    )
    trace = jnp.sum(jnp.where(eye, gram, 0.0))
    inverse = 1.0 / (jnp.sqrt(jnp.full((1, 1), trace, F32)) + epsilon)
    gram = gram * inverse * inverse

    def poly(g, low):
        return (
            jnp.where(eye, coef_a, 0.0) + coef_b * g + coef_c * dot(low, low)
        ).astype(BF)

    low = gram.astype(BF)
    p1 = poly(gram, low)
    gram = dot(p1, dot(low, p1).astype(BF))
    low = gram.astype(BF)
    p2 = poly(gram, low)
    q = dot(p1, p2).astype(BF)
    gram = dot(p2, dot(low, p2).astype(BF))
    p3 = poly(gram, gram.astype(BF))
    q = (dot(q, p3) * inverse).astype(BF)

    me = lax.axis_index(AXIS)
    high, corner = me // 4, me % 4
    at = 0
    for flip, parts in flips:
        for dist in parts:
            block = (high ^ dist) * 4 + (corner ^ flip)
            start = pl.multiple_of(block * share, share)
            outs[at][...] = dot(m_ref[pl.ds(start, share), :], q).astype(BF)
            at += 1


def orthogonal(gram, moment, flips):
    rows, cols = moment.shape
    count = lax.axis_size(AXIS)
    share = rows // count
    total = sum(len(parts) for _, parts in flips)
    return pl.pallas_call(
        functools.partial(ortho_body, share, count // 4, flips),
        grid=(1,),
        out_shape=[jax.ShapeDtypeStruct((share, cols), BF)] * total,
        in_specs=[whole((cols, cols)), whole((rows, cols))],
        out_specs=[whole((share, cols))] * total,
        cost_estimate=cost(
            18 * cols**3 + 2 * total * share * cols * cols, 4 * cols * cols + 4 * rows * cols
        ),
        name="ortho",
    )(gram, moment)


def add_body(*refs):
    total = refs[0][...].astype(F32)
    for ref in refs[1:-1]:
        total = total + ref[...].astype(F32)
    refs[-1][...] = total.astype(BF)


def add_all(*blocks):
    shape = blocks[0].shape
    return pl.pallas_call(
        add_body,
        grid=(1,),
        out_shape=jax.ShapeDtypeStruct(shape, BF),
        in_specs=[whole(shape)] * len(blocks),
        out_specs=whole(shape),
        cost_estimate=cost(math.prod(shape) * len(blocks), 2 * math.prod(shape) * len(blocks)),
        name="add",
    )(*blocks)


def outer_body(scale, share, count, *refs):
    terms, (w_ref, outer_ref, fresh_ref, new_ref) = refs[:count], refs[count:]
    total = terms[0][...].astype(F32)
    for ref in terms[1:]:
        total = total + ref[...].astype(F32)
    fresh = outer_beta * outer_ref[...] + scale * total
    fresh_ref[...] = fresh
    start = pl.multiple_of(lax.axis_index(AXIS) * share, share)
    own = w_ref[pl.ds(start, share), :].astype(F32)
    new_ref[...] = (own - outer_rate * fresh).astype(BF)


def outer_step(terms, weights, outer, scale):
    share, cols = outer.shape
    block = whole((share, cols))
    return pl.pallas_call(
        functools.partial(outer_body, scale, share, len(terms)),
        grid=(1,),
        out_shape=[
            jax.ShapeDtypeStruct((share, cols), F32),
            jax.ShapeDtypeStruct((share, cols), BF),
        ],
        in_specs=[block] * len(terms) + [whole(weights.shape), block],
        out_specs=[block, block],
        cost_estimate=cost(8 * share * cols, 20 * share * cols),
        name="outer",
    )(*terms, weights, outer)


def place_body(share, dists, aliased, *refs):
    blocks, out, sems = refs[: len(dists)], refs[-2], refs[-1]
    me = lax.axis_index(AXIS)
    copies = []
    for i, dist in enumerate(dists):
        start = pl.multiple_of((me ^ dist) * share, share)
        copies.append(
            pltpu.make_async_copy(blocks[i], out.at[pl.ds(start, share), :], sems.at[i])
        )
    for copy in copies:
        copy.start()
    for copy in copies:
        copy.wait()


def place(blocks, dists, onto, rows):
    share, cols = blocks[0].shape
    aliased = onto is not None
    return pl.pallas_call(
        functools.partial(place_body, share, dists, aliased),
        grid=(1,),
        out_shape=jax.ShapeDtypeStruct((rows, cols), BF),
        in_specs=[whole((share, cols))] * len(blocks) + [ANY] * aliased,
        out_specs=ANY,
        scratch_shapes=[pltpu.SemaphoreType.DMA((len(blocks),))],
        input_output_aliases={len(blocks): 0} if aliased else {},
        cost_estimate=cost(1, 4 * share * cols * len(blocks)),
        name="place",
    )(*blocks, *([onto] if aliased else []))


def per_device(weights, momentum, gradients, outer_momentum):
    count = lax.axis_size(AXIS)
    rows, cols = weights.shape[-2:]
    moment = momentum.reshape(rows, cols)
    grads = gradients.reshape(2, rows, cols)
    weights2 = weights.reshape(rows, cols)
    outer = outer_momentum.reshape(outer_momentum.shape[-2:])

    own0 = prepare(moment, grads, [0]) + prepare(moment, grads, list(range(1, CHUNKS)))
    state = dict(rows=rows, cols=cols, own0=own0, own1=[], got1=[])
    state["got0"] = [swap(block, 1) for block in own0]
    groups = count // 4
    others = tuple(range(1, groups))
    order = others + (0,)
    for j in range(CHUNKS + LAG):
        tick(j, state, grads)
        if j < CHUNKS:
            state["got1"].append(swap(state["own1"][j], 2))
        if j == CHUNKS - 1:
            first = orthogonal(state["g0"], state["m0"], ((2, order), (0, order)))
            there = [swap(block, 2) for block in first[:groups]]
    second = orthogonal(state["g1"], state["m1"], ((1, order), (0, order)))
    across = [swap(block, 1) for block in second[:groups]]
    terms = [
        (first[groups + i], there[i], second[groups + i], across[i]) for i in range(groups)
    ]
    sums = [swap(add_all(*terms[i]), 4 * dist) for i, dist in enumerate(others)]
    scale = 0.5 * 0.2 * math.sqrt(rows) * 2 / count
    fresh, own = outer_step((*terms[-1], *sums), weights2, outer, scale)

    known = {0: own}
    for bit in reversed(range(count.bit_length() - 1)):
        for dist in sorted(known):
            known[dist | 1 << bit] = swap(known[dist], 1 << bit)
    dists = sorted(known)
    result = place([known[d] for d in dists[:-1]], dists[:-1], None, rows)
    result = place([known[dists[-1]]], dists[-1:], result, rows)
    return (result.reshape(weights.shape), fresh.reshape(outer_momentum.shape))


def solution(mesh):
    count = mesh.shape[AXIS]
    if count < 4 or count & (count - 1):
        raise ValueError("replica count")
    in_specs = (
        P("expert", None, None),
        P("replica", "expert", None, None),
        P(None, "replica", "expert", None, None),
        P("expert", "replica", None),
    )
    out_specs = (P("expert", None, None), P("expert", "replica", None))
    return jax.shard_map(
        per_device, mesh=mesh, in_specs=in_specs, out_specs=out_specs, check_vma=False
    )
```

```python
import functools
import math

import jax
import jax.numpy as jnp
from jax import lax
from jax.experimental import pallas as pl
from jax.experimental.pallas import tpu as pltpu
from jax.sharding import PartitionSpec as P

AXIS = "replica"
CHUNKS = 8
LAG = 2

coef_a = 3.4445
coef_b = -4.775
coef_c = 2.0315
inner_beta = 0.9
outer_beta = 0.9
outer_rate = 1.0
epsilon = 1e-07

BF = jnp.bfloat16
F32 = jnp.float32


def swap(block, mask):
    count = lax.axis_size(AXIS)
    return lax.ppermute(block, AXIS, [(i, i ^ mask) for i in range(count)])


def gram_of(block):
    return lax.dot_general(
        block, block, (((0,), (0,)), ((), ())), preferred_element_type=F32
    )


def dot(left, right):
    return jnp.dot(left, right, preferred_element_type=F32)


def whole(shape):
    return pl.BlockSpec(shape, lambda i: (0,) * len(shape))


ANY = pl.BlockSpec(memory_space=pl.ANY)


LIGHT = pltpu.CompilerParams(vmem_limit_bytes=16 << 20)


def cost(flops, nbytes):
    return pl.CostEstimate(flops=int(flops), bytes_accessed=int(nbytes), transcendentals=0)


def prep_body(count, *refs):
    ins, outs = refs[: 2 * count], refs[2 * count :]
    for i in range(count):
        outs[i][...] = (
            inner_beta * ins[2 * i][...] + ins[2 * i + 1][...].astype(F32)
        ).astype(BF)


def prepare(moment, grads, chunks):
    rows, cols = moment.shape
    n = rows // CHUNKS
    specs, args = [], []
    for k in chunks:
        specs.append(pl.BlockSpec((n, cols), lambda i, k=k: (k, 0)))
        specs.append(pl.BlockSpec((None, n, cols), lambda i, k=k: (0, k, 0)))
        args += [moment, grads]
    return pl.pallas_call(
        functools.partial(prep_body, len(chunks)),
        grid=(1,),
        out_shape=[jax.ShapeDtypeStruct((n, cols), BF)] * len(chunks),
        in_specs=specs,
        out_specs=[whole((n, cols))] * len(chunks),
        cost_estimate=cost(2 * n * cols * len(chunks), 8 * n * cols * len(chunks)),
        compiler_params=LIGHT,
        name="prep",
    )(*args)


def tick_body(first, last, names, *refs):
    ref = dict(zip(names, refs))
    if first:
        mean = 0.5 * (ref["own0"][...].astype(F32) + ref["got0"][...].astype(F32))
        low = mean.astype(BF)
        ref["m0"][...] = low
        ref["send"][...] = (inner_beta * mean + ref["grad"][...].astype(F32)).astype(BF)
        gram = gram_of(low)
        ref["g0"][...] = gram + ref["g0in"][...] if "g0in" in ref else gram
    if last:
        low = (
            0.5 * (ref["own1"][...].astype(F32) + ref["got1"][...].astype(F32))
        ).astype(BF)
        ref["m1"][...] = low
        gram = gram_of(low)
        ref["g1"][...] = gram + ref["g1in"][...] if "g1in" in ref else gram


def tick(j, state, grads):
    rows, cols = state["rows"], state["cols"]
    n = rows // CHUNKS
    chunk = whole((n, cols))
    square = whole((cols, cols))
    names, specs, args = [], [], []
    onames, ospecs, oshapes = [], [], []
    alias = {}

    def put(name, spec, value):
        names.append(name)
        specs.append(spec)
        args.append(value)

    def out(name, spec, shape, dtype, onto=None):
        if onto is not None:
            alias[names.index(onto)] = len(onames)
        onames.append(name)
        ospecs.append(spec)
        oshapes.append(jax.ShapeDtypeStruct(shape, dtype))

    first, last = j < CHUNKS, j >= LAG
    if first:
        put("own0", chunk, state["own0"][j])
        put("got0", chunk, state["got0"][j])
        put("grad", pl.BlockSpec((None, n, cols), lambda i: (1, j, 0)), grads)
        if j > 0:
            put("g0in", square, state["g0"])
            put("m0in", ANY, state["m0"])
    if last:
        i = j - LAG
        put("own1", chunk, state["own1"][i])
        put("got1", chunk, state["got1"][i])
        if i > 0:
            put("g1in", square, state["g1"])
            put("m1in", ANY, state["m1"])
    if first:
        place = pl.BlockSpec((n, cols), lambda i: (j, 0))
        out("m0", place, (rows, cols), BF, "m0in" if j > 0 else None)
        out("send", chunk, (n, cols), BF)
        out("g0", square, (cols, cols), F32, "g0in" if j > 0 else None)
    if last:
        place = pl.BlockSpec((n, cols), lambda i: (j - LAG, 0))
        out("m1", place, (rows, cols), BF, "m1in" if i > 0 else None)
        out("g1", square, (cols, cols), F32, "g1in" if i > 0 else None)
    results = pl.pallas_call(
        functools.partial(tick_body, first, last, names + onames),
        grid=(1,),
        out_shape=oshapes,
        in_specs=specs,
        out_specs=ospecs,
        input_output_aliases=alias,
        cost_estimate=cost(4 * n * cols * cols, 8 * cols * cols + 10 * n * cols),
        compiler_params=LIGHT,
        name="tick",
    )(*args)
    got = dict(zip(onames, results))
    if first:
        state["own1"].append(got.pop("send"))
    state.update(got)


def ortho_body(share, groups, flips, gram_ref, m_ref, *outs):
    gram = gram_ref[...]
    size = gram.shape[0]
    eye = lax.broadcasted_iota(jnp.int32, (size, size), 0) == lax.broadcasted_iota(
        jnp.int32, (size, size), 1
    )
    trace = jnp.sum(jnp.where(eye, gram, 0.0))
    inverse = 1.0 / (jnp.sqrt(jnp.full((1, 1), trace, F32)) + epsilon)
    gram = gram * inverse * inverse

    def poly(g, low):
        return (
            jnp.where(eye, coef_a, 0.0) + coef_b * g + coef_c * dot(low, low)
        ).astype(BF)

    low = gram.astype(BF)
    p1 = poly(gram, low)
    gram = dot(p1, dot(low, p1).astype(BF))
    low = gram.astype(BF)
    p2 = poly(gram, low)
    q = dot(p1, p2).astype(BF)
    gram = dot(p2, dot(low, p2).astype(BF))
    p3 = poly(gram, gram.astype(BF))
    q = (dot(q, p3) * inverse).astype(BF)

    me = lax.axis_index(AXIS)
    high, corner = me // 4, me % 4
    at = 0
    for flip, parts in flips:
        for dist in parts:
            block = (high ^ dist) * 4 + (corner ^ flip)
            start = pl.multiple_of(block * share, share)
            outs[at][...] = dot(m_ref[pl.ds(start, share), :], q).astype(BF)
            at += 1


def orthogonal(gram, moment, flips):
    rows, cols = moment.shape
    count = lax.axis_size(AXIS)
    share = rows // count
    total = sum(len(parts) for _, parts in flips)
    return pl.pallas_call(
        functools.partial(ortho_body, share, count // 4, flips),
        grid=(1,),
        out_shape=[jax.ShapeDtypeStruct((share, cols), BF)] * total,
        in_specs=[whole((cols, cols)), whole((rows, cols))],
        out_specs=[whole((share, cols))] * total,
        cost_estimate=cost(
            18 * cols**3 + 2 * total * share * cols * cols, 4 * cols * cols + 4 * rows * cols
        ),
        compiler_params=LIGHT,
        name="ortho",
    )(gram, moment)


def add_body(*refs):
    total = refs[0][...].astype(F32)
    for ref in refs[1:-1]:
        total = total + ref[...].astype(F32)
    refs[-1][...] = total.astype(BF)


def add_all(*blocks):
    shape = blocks[0].shape
    return pl.pallas_call(
        add_body,
        grid=(1,),
        out_shape=jax.ShapeDtypeStruct(shape, BF),
        in_specs=[whole(shape)] * len(blocks),
        out_specs=whole(shape),
        cost_estimate=cost(math.prod(shape) * len(blocks), 2 * math.prod(shape) * len(blocks)),
        compiler_params=LIGHT,
        name="add",
    )(*blocks)


def outer_body(scale, share, count, *refs):
    terms, (w_ref, outer_ref, fresh_ref, new_ref) = refs[:count], refs[count:]
    total = terms[0][...].astype(F32)
    for ref in terms[1:]:
        total = total + ref[...].astype(F32)
    fresh = outer_beta * outer_ref[...] + scale * total
    fresh_ref[...] = fresh
    start = pl.multiple_of(lax.axis_index(AXIS) * share, share)
    own = w_ref[pl.ds(start, share), :].astype(F32)
    new_ref[...] = (own - outer_rate * fresh).astype(BF)


def outer_step(terms, weights, outer, scale):
    share, cols = outer.shape
    block = whole((share, cols))
    return pl.pallas_call(
        functools.partial(outer_body, scale, share, len(terms)),
        grid=(1,),
        out_shape=[
            jax.ShapeDtypeStruct((share, cols), F32),
            jax.ShapeDtypeStruct((share, cols), BF),
        ],
        in_specs=[block] * len(terms) + [whole(weights.shape), block],
        out_specs=[block, block],
        cost_estimate=cost(8 * share * cols, 20 * share * cols),
        compiler_params=LIGHT,
        name="outer",
    )(*terms, weights, outer)


def place_body(share, dists, aliased, *refs):
    blocks, out, sems = refs[: len(dists)], refs[-2], refs[-1]
    me = lax.axis_index(AXIS)
    copies = []
    for i, dist in enumerate(dists):
        start = pl.multiple_of((me ^ dist) * share, share)
        copies.append(
            pltpu.make_async_copy(blocks[i], out.at[pl.ds(start, share), :], sems.at[i])
        )
    for copy in copies:
        copy.start()
    for copy in copies:
        copy.wait()


def place(blocks, dists, onto, rows):
    share, cols = blocks[0].shape
    aliased = onto is not None
    return pl.pallas_call(
        functools.partial(place_body, share, dists, aliased),
        grid=(1,),
        out_shape=jax.ShapeDtypeStruct((rows, cols), BF),
        in_specs=[whole((share, cols))] * len(blocks) + [ANY] * aliased,
        out_specs=ANY,
        scratch_shapes=[pltpu.SemaphoreType.DMA((len(blocks),))],
        input_output_aliases={len(blocks): 0} if aliased else {},
        cost_estimate=cost(1, 4 * share * cols * len(blocks)),
        compiler_params=LIGHT,
        name="place",
    )(*blocks, *([onto] if aliased else []))


def per_device(weights, momentum, gradients, outer_momentum):
    count = lax.axis_size(AXIS)
    rows, cols = weights.shape[-2:]
    moment = momentum.reshape(rows, cols)
    grads = gradients.reshape(2, rows, cols)
    weights2 = weights.reshape(rows, cols)
    outer = outer_momentum.reshape(outer_momentum.shape[-2:])

    own0 = prepare(moment, grads, [0]) + prepare(moment, grads, list(range(1, CHUNKS)))
    state = dict(rows=rows, cols=cols, own0=own0, own1=[], got1=[])
    state["got0"] = [swap(block, 1) for block in own0]
    groups = count // 4
    others = tuple(range(1, groups))
    order = others + (0,)
    for j in range(CHUNKS + LAG):
        tick(j, state, grads)
        if j < CHUNKS:
            state["got1"].append(swap(state["own1"][j], 2))
        if j == CHUNKS - 1:
            first = orthogonal(state["g0"], state["m0"], ((2, order), (0, order)))
            there = [swap(block, 2) for block in first[:groups]]
    second = orthogonal(state["g1"], state["m1"], ((1, order), (0, order)))
    across = [swap(block, 1) for block in second[:groups]]
    terms = [
        (first[groups + i], there[i], second[groups + i], across[i]) for i in range(groups)
    ]
    sums = [swap(add_all(*terms[i]), 4 * dist) for i, dist in enumerate(others)]
    scale = 0.5 * 0.2 * math.sqrt(rows) * 2 / count
    fresh, own = outer_step((*terms[-1], *sums), weights2, outer, scale)

    known = {0: own}
    for bit in reversed(range(count.bit_length() - 1)):
        for dist in sorted(known):
            known[dist | 1 << bit] = swap(known[dist], 1 << bit)
    dists = sorted(known)
    result = place([known[d] for d in dists[:-1]], dists[:-1], None, rows)
    result = place([known[dists[-1]]], dists[-1:], result, rows)
    return (result.reshape(weights.shape), fresh.reshape(outer_momentum.shape))


def solution(mesh):
    count = mesh.shape[AXIS]
    if count < 4 or count & (count - 1):
        raise ValueError("replica count")
    in_specs = (
        P("expert", None, None),
        P("replica", "expert", None, None),
        P(None, "replica", "expert", None, None),
        P("expert", "replica", None),
    )
    out_specs = (P("expert", None, None), P("expert", "replica", None))
    return jax.shard_map(
        per_device, mesh=mesh, in_specs=in_specs, out_specs=out_specs, check_vma=False
    )
```
